32 devices in a mesh: dom: 16 (over z, y, core), col: 2 (over x).
Axes of the slice: x: 2, y: 2, z: 4, core: 2. Of those that a mesh axis runs over, the one named last changes fastest.
Arguments:
- wave: float32 [65536, 32], P(('dom', 'col')), may hold values from -6 to 6
- mass_scale: float32 [65536], P(('dom', 'col')), may hold values from 0.5 to 2
- potential: float32 [65536], P(('dom', 'col')), may hold values from -1 to 1
- stiffness: float32 [125, 125], replicated
- cell_scale: float32 [1024], P(('dom', 'col')), may hold values from 0.5 to 2
- cell_map: int32 [125, 1024], P(None, ('dom', 'col')), may hold values from 0 to 3071, as said below
- send_left: int32 [16384], P(('dom', 'col')), may hold values from 0 to 2047
- send_right: int32 [16384], P(('dom', 'col')), may hold values from 0 to 2047
- support_node: int32 [16384], P(('dom', 'col')), may hold values from 0 to 2047
- support_atom: int32 [16384], P(('dom', 'col')), may hold values from 0 to 20, as said below
- projector: float32 [8, 16384], P(None, ('dom', 'col')), may hold values from -1 to 1
- coupling: float32 [8, 320], P(None, 'dom'), may hold values from 0.25 to 1.5
Outputs:
- filtered: float32 [65536, 32], P(('dom', 'col'))
The draws below stay inside these ranges and needn't reach their ends.
Inputs may be any that keep to these rules, and one draw needn't show every extreme that they name: `cell_map`: local node numbers of the cell's partition: below 2048 an owned node, 2048 + i the i-th row received from the previous partition, 2560 + i the i-th row from the next one. The cells of a partition with local number below 24 name owned nodes only. `send_left`: local owned node numbers. `send_right`: local owned node numbers. `support_node`: local owned node numbers. `support_atom`: atom number within the neighbourhood; 20 marks an empty slot. A partition's empty slots follow its live ones, and some partition has none.
All inputs are finite; a program needn't handle non-finite values.
Results may differ from the reference program's by a relative error of at most 0.0003.
Values sent between devices are 32-bit elements; how exact they have to be, the bound alone decides.
A program may use at most 64 MiB of HBM per device.

```python
import math
import jax
import jax.numpy as jnp
from jax import lax

CELL_NODES = 125
COLS = 32
NPROJ = 8
NODES_DEV = 2048
CELLS_DEV = 32
GHOST = 512
SUPP_DEV = 512
ATOMS_GRP = 20
NODES = 65536
CELLS = 1024
GHOSTS_ALL = 16384
SUPP = 16384
ATOMS = 320
N_DOM = 16
N_COL = 2


def draw_stiffness(key, part):
    base = jax.random.normal(key, (CELL_NODES, CELL_NODES), jnp.float32)
    symmetric = (base + base.T) * (0.5 / math.sqrt(CELL_NODES))
    return symmetric + 1.5 * jnp.eye(CELL_NODES, dtype=jnp.float32)


def draw_cell_map(key, part):
    first_key, second_key, third_key = jax.random.split(jax.random.fold_in(key, 11), 3)
    owned_nodes = jax.random.randint(first_key, (CELL_NODES, CELLS), 0, NODES_DEV)
    ghost_nodes = jax.random.randint(second_key, (CELL_NODES, CELLS), NODES_DEV, NODES_DEV + 2 * GHOST)
    picker = jax.random.randint(third_key, (CELL_NODES, CELLS), 0, 2)
    position = jnp.arange(CELLS, dtype=jnp.int32) % CELLS_DEV
    boundary = (position >= CELLS_DEV - CELLS_DEV // 4)[None, :]
    return jnp.where(boundary & (picker == 1), ghost_nodes, owned_nodes).astype(jnp.int32)


def draw_support_atom(key, part):
    first_key, second_key = jax.random.split(jax.random.fold_in(key, 23), 2)
    live_counts = jax.random.randint(first_key, (N_DOM * N_COL,), SUPP_DEV // 4, SUPP_DEV + 1)
    live_counts = live_counts.at[0].set(SUPP_DEV)
    atom_draw = jax.random.randint(second_key, (SUPP,), 0, ATOMS_GRP)
    position = jnp.arange(SUPP, dtype=jnp.int32) % SUPP_DEV
    owner = jnp.arange(SUPP, dtype=jnp.int32) // SUPP_DEV
    return jnp.where(position < live_counts[owner], atom_draw, ATOMS_GRP).astype(jnp.int32)


def with_ends(entries, rng, low, top_value):
    place = [jax.random.randint(jax.random.fold_in(rng, axis), (), 0, length) for axis, length in enumerate(entries.shape)]
    main_axis = entries.shape.index(max(entries.shape))
    next_to = place[:main_axis] + [(place[main_axis] + 1) % entries.shape[main_axis]] + place[main_axis + 1:]
    return entries.at[tuple(place)].set(low).at[tuple(next_to)].set(top_value)


def levels(rng, extent, cuts, low, top_value):
    def one(dim, blocks):
        steps = jax.random.uniform(jax.random.fold_in(jax.random.fold_in(rng, 6), dim), (blocks,), jnp.float32, low / len(cuts), top_value / len(cuts))
        return jnp.repeat(jnp.exp(steps), extent[dim] // blocks).reshape((-1,) + (1,) * (len(extent) - dim - 1))

    gain = one(*cuts[0])
    for cut in cuts[1:]:
        gain = gain * one(*cut)
    return gain


def centred(key, shape, scale, most, cuts=(), kind=jnp.bfloat16):
    array = jax.random.normal(key, shape, jnp.float32) * scale
    if len(cuts) > 0:
        array = levels(key, shape, cuts, -0.22, 0.18) * array
    return jnp.clip(array, min=-most, max=most).astype(kind)


def setup_inputs(seed: int = 0) -> dict:
    key_of = jax.random.split(jax.random.key(seed), 13)
    wave = centred(key_of[0], (NODES, COLS), 1.0, 6.0, ((0, 32),), jnp.float32)
    mass_scale = jnp.clip(jnp.exp(math.log(2.0) - 1.3862944 * jax.random.uniform(key_of[1], (NODES,), jnp.float32) ** levels(key_of[1], (NODES,), ((0, 32),), -0.2, 0.2)), 0.5, 2.0)
    potential = jnp.clip(jax.random.uniform(key_of[2], (NODES,), jnp.float32, -1.0, 1.0) * levels(key_of[2], (NODES,), ((0, 32),), -0.4, 0.0), -1.0, 1.0)
    stiffness = draw_stiffness(jax.random.fold_in(key_of[12], 71), 0)
    cell_scale = jnp.clip(jnp.exp(math.log(2.0) - 1.3862944 * jax.random.uniform(key_of[4], (CELLS,), jnp.float32) ** levels(key_of[4], (CELLS,), ((0, 32),), -0.2, 0.2)), 0.5, 2.0)
    cell_map = draw_cell_map(jax.random.fold_in(key_of[12], 71), 0)
    send_left = with_ends(jax.random.randint(key_of[6], (GHOSTS_ALL,), 0, NODES_DEV), jax.random.fold_in(key_of[6], 1), 0, NODES_DEV - 1).astype(jnp.int32)
    send_right = with_ends(jax.random.randint(key_of[7], (GHOSTS_ALL,), 0, NODES_DEV), jax.random.fold_in(key_of[7], 1), 0, NODES_DEV - 1).astype(jnp.int32)
    support_node = with_ends(jax.random.randint(key_of[8], (SUPP,), 0, NODES_DEV), jax.random.fold_in(key_of[8], 1), 0, NODES_DEV - 1).astype(jnp.int32)
    support_atom = draw_support_atom(jax.random.fold_in(key_of[12], 71), 0)
    projector = centred(key_of[10], (NPROJ, SUPP), 0.15, 1.0, ((1, 32),), jnp.float32)
    coupling = jnp.clip(0.25 + 1.25 * jax.random.uniform(key_of[11], (NPROJ, ATOMS), jnp.float32) ** levels(key_of[11], (NPROJ, ATOMS), ((1, 16),), -0.2, 0.2), 0.25, 1.5)
    return {"wave": wave, "mass_scale": mass_scale, "potential": potential, "stiffness": stiffness, "cell_scale": cell_scale, "cell_map": cell_map, "send_left": send_left, "send_right": send_right, "support_node": support_node, "support_atom": support_atom, "projector": projector, "coupling": coupling}


def reference(wave, mass_scale, potential, stiffness, cell_scale, cell_map, send_left, send_right, support_node, support_atom, projector, coupling):
    parts = N_DOM * N_COL
    highest = lax.Precision.HIGHEST
    left_lists = send_left.reshape(parts, GHOST)
    right_lists = send_right.reshape(parts, GHOST)
    maps = cell_map.reshape(CELL_NODES, parts, CELLS_DEV).transpose(1, 0, 2)
    scales = cell_scale.reshape(parts, CELLS_DEV)
    slot_nodes = support_node.reshape(parts, SUPP_DEV)
    slot_atoms = support_atom.reshape(parts, SUPP_DEV)
    slot_values = projector.reshape(NPROJ, parts, SUPP_DEV).transpose(1, 0, 2)
    couple = coupling.reshape(NPROJ, N_DOM, ATOMS_GRP).transpose(1, 2, 0)
    atom_ids = jnp.arange(ATOMS_GRP, dtype=jnp.int32)
    take_rows = jax.vmap(lambda block, index: block[index])
    add_rows = jax.vmap(lambda block, index, extra: block.at[index].add(extra))
    zero_block = jnp.zeros((1, GHOST, COLS), jnp.float32)

    def cell_part(operands):
        extended, local_map, local_scale = operands
        gathered = extended[local_map]
        product = jnp.dot(stiffness, gathered.reshape(CELL_NODES, -1), precision=highest, preferred_element_type=jnp.float32)
        product = product.reshape(gathered.shape) * local_scale[None, :, None]
        return jnp.zeros_like(extended).at[local_map].add(product)

    def project_part(operands):
        block, nodes_here, atoms_here, values_here = operands
        onehot = (atoms_here[:, None] == atom_ids[None, :]).astype(jnp.float32)
        return jnp.einsum("ea,je,ek->ajk", onehot, values_here, block[nodes_here], precision=highest)

    def spread_part(operands):
        block, nodes_here, atoms_here, values_here, coeff_here = operands
        onehot = (atoms_here[:, None] == atom_ids[None, :]).astype(jnp.float32)
        back = jnp.einsum("ea,je,ajk->ek", onehot, values_here, coeff_here, precision=highest)
        return block.at[nodes_here].add(back)

    def apply_ham(field):
        scaled = (mass_scale[:, None] * field).reshape(parts, NODES_DEV, COLS)
        to_left = take_rows(scaled, left_lists)
        to_right = take_rows(scaled, right_lists)
        from_left = jnp.concatenate([zero_block, to_right[:-1]], axis=0)
        from_right = jnp.concatenate([to_left[1:], zero_block], axis=0)
        extended = jnp.concatenate([scaled, from_left, from_right], axis=1)
        assembled = lax.map(cell_part, (extended, maps, scales))
        folded = assembled[:, :NODES_DEV]
        back_left = assembled[:, NODES_DEV:NODES_DEV + GHOST]
        back_right = assembled[:, NODES_DEV + GHOST:]
        folded = add_rows(folded, right_lists, jnp.concatenate([back_left[1:], zero_block], axis=0))
        folded = add_rows(folded, left_lists, jnp.concatenate([zero_block, back_right[:-1]], axis=0))
        projections = lax.map(project_part, (scaled, slot_nodes, slot_atoms, slot_values))
        summed = projections.reshape(N_DOM, N_COL, ATOMS_GRP, NPROJ, COLS).sum(axis=1)
        coefficients = summed * couple[:, :, :, None]
        per_part = jnp.broadcast_to(coefficients[:, None], (N_DOM, N_COL, ATOMS_GRP, NPROJ, COLS)).reshape(parts, ATOMS_GRP, NPROJ, COLS)
        nonlocal_sum = lax.map(spread_part, (folded, slot_nodes, slot_atoms, slot_values, per_part))
        return mass_scale[:, None] * nonlocal_sum.reshape(NODES, COLS) + potential[:, None] * field

    first = (apply_ham(wave) - 2.0 * wave) / 4.0
    return 2.0 * (apply_ham(first) - 2.0 * first) / 4.0 - wave
```

```python
import functools

import jax
import jax.numpy as jnp
from jax import lax
from jax.experimental import pallas as pl
from jax.experimental.pallas import tpu as pltpu
from jax.sharding import PartitionSpec as P

L = 128
BF = jnp.bfloat16
F32 = jnp.float32
MESH = pl.DeviceIdType.MESH


def split(x):
    hi = x.astype(BF)
    return hi, (x - hi.astype(F32)).astype(BF)


def dot(a, b):
    return jnp.dot(a, b, preferred_element_type=F32)


def kernel(
    cfg,
    wave_ref, mass_ref, pot_ref, stiff_ref, scale_ref, map_ref,
    left_ref, right_ref, node_ref, atom_ref, proj_ref, coup_ref,
    out_ref,
    field, vcur, vwave, mass, pot, smat, cellrow,
    ohi, ohb, ohs, otm, otg, mask, z, acc,
    paf, pa, pat, cpl, coef,
    halo_send, halo_recv, back_send, back_recv, proj_send, proj_recv,
    hs_sem, hr_sem, bs_sem, br_sem, ps_sem, pr_sem,
):
    n_dom, n_col = cfg["n_dom"], cfg["n_col"]
    cols, groups, rows = cfg["cols"], cfg["groups"], cfg["rows"]
    cells, inner, width = cfg["cells"], cfg["inner"], cfg["cell_nodes"]
    nodes, ghost, slots = cfg["nodes"], cfg["ghost"], cfg["slots"]
    atoms, nproj = cfg["atoms"], cfg["nproj"]
    grows = ghost // groups
    tiles = rows // L
    sup0 = cells * L
    fold0 = sup0 + slots
    total = fold0 + 2 * ghost
    arows = atoms * nproj
    apad = paf.shape[0]

    dom = lax.axis_index("dom")
    col = lax.axis_index("col")
    me = dom * n_col + col
    last = n_dom * n_col - 1
    has_prev = me > 0
    has_next = me < last
    prev = jnp.maximum(me - 1, 0)
    after = jnp.minimum(me + 1, last)
    prev_id = (prev // n_col, prev % n_col)
    next_id = (after // n_col, after % n_col)
    outer_prev = jnp.logical_and(has_prev, col == 0)
    outer_next = jnp.logical_and(has_next, col == n_col - 1)

    zero_block = jnp.zeros((grows, L), F32)
    for it in range(2):
        @pl.when(jnp.logical_not(has_prev))
        def _():
            halo_recv[it, 0] = zero_block
            back_recv[it, 0] = zero_block

        @pl.when(jnp.logical_not(has_next))
        def _():
            halo_recv[it, 1] = zero_block
            back_recv[it, 1] = zero_block

    barrier = pltpu.get_barrier_semaphore()
    for k in range(1, n_col):
        pl.semaphore_signal(
            barrier, inc=1, device_id=(dom, (col + k) % n_col), device_id_type=MESH
        )

    @pl.when(outer_prev)
    def _():
        pl.semaphore_signal(barrier, inc=1, device_id=prev_id, device_id_type=MESH)

    @pl.when(outer_next)
    def _():
        pl.semaphore_signal(barrier, inc=1, device_id=next_id, device_id_type=MESH)

    lane = lax.broadcasted_iota(jnp.int32, (L, L), 1)
    sub = lax.broadcasted_iota(jnp.int32, (L, L), 0)
    lane_group = lane // cols

    def replicate(x):
        shift = L // 2
        while shift >= cols:
            x = x + pltpu.roll(x, shift, 1)
            shift //= 2
        return x

    for t in range(tiles):
        block = jnp.concatenate(
            [wave_ref[:, q * rows + t * L : q * rows + (t + 1) * L] for q in range(groups)], axis=0
        )
        block = block.T
        vcur[t * L : (t + 1) * L, :] = block
        vwave[t * L : (t + 1) * L, :] = block
        for source, target in ((mass_ref, mass), (pot_ref, pot)):
            block = jnp.concatenate(
                [
                    jnp.broadcast_to(source[q * tiles + t : q * tiles + t + 1, :], (cols, L))
                    for q in range(groups)
                ],
                axis=0,
            )
            target[t * L : (t + 1) * L, :] = block.T

    acc[0:L, 0:L] = jnp.zeros((L, L), F32)
    acc[0:width, 0:width] = stiff_ref[...]
    s_hi, s_lo = split(acc[0:L, 0:L])
    smat[:, 0:L] = s_hi
    smat[:, L : 2 * L] = s_lo

    cellrow[...] = jnp.full((cells, L), -1, jnp.int32)
    cellrow[:, 0:width] = map_ref[...]

    def place(n):
        g = n - nodes
        hi = jnp.where(
            g < 0,
            jnp.where(n < 0, -1, n % rows),
            rows + (g // ghost) * grows + g % grows,
        )
        q = jnp.where(g < 0, n // rows, (g // grows) % groups)
        return hi, q

    def onehot(condition):
        return jnp.where(condition, 1.0, 0.0).astype(BF)

    def tables(row, at, gather_ref, gather_at, ghosts_ref=None, ghosts_at=0):
        wide = jnp.broadcast_to(row, (L, L))
        hi_r, _ = place(wide)
        hi_c, q_c = place(wide.T)
        for t in range(gather_ref.shape[1] // L):
            gather_ref[pl.ds(gather_at, L), t * L : (t + 1) * L] = onehot(hi_c == lane + t * L)
        mask[pl.ds(at, L), :] = onehot(q_c == lane_group)
        for t in range(tiles):
            otm[t * L : (t + 1) * L, pl.ds(at, L)] = onehot(hi_r == sub + t * L)
        if ghosts_ref is not None:
            for t in range(2 * grows // L):
                ghosts_ref[t * L : (t + 1) * L, pl.ds(ghosts_at, L)] = onehot(
                    hi_r == sub + (rows + t * L)
                )

    for k, ref in enumerate((left_ref, right_ref, node_ref)):
        base = (fold0, fold0 + ghost, sup0)[k]
        for t in range(ref.shape[0]):
            tables(ref[t : t + 1, :], base + t * L, ohs, k * ghost + t * L)

    pl.semaphore_wait(
        barrier, n_col - 1 + jnp.where(outer_prev, 1, 0) + jnp.where(outer_next, 1, 0)
    )

    def halo_copy(it, side):
        return pltpu.make_async_remote_copy(
            src_ref=halo_send.at[it, side], dst_ref=halo_recv.at[it, 1 - side],
            send_sem=hs_sem.at[it, side], recv_sem=hr_sem.at[it, 1 - side],
            device_id=(prev_id, next_id)[side], device_id_type=MESH,
        )

    def back_copy(it, side):
        return pltpu.make_async_remote_copy(
            src_ref=back_send.at[it, side], dst_ref=back_recv.at[it, 1 - side],
            send_sem=bs_sem.at[it, side], recv_sem=br_sem.at[it, 1 - side],
            device_id=(prev_id, next_id)[side], device_id_type=MESH,
        )

    def proj_copy(it, k):
        return pltpu.make_async_remote_copy(
            src_ref=proj_send.at[it], dst_ref=proj_recv.at[it, k - 1],
            send_sem=ps_sem.at[it, k - 1], recv_sem=pr_sem.at[it, k - 1],
            device_id=(dom, (col + k) % n_col), device_id_type=MESH,
        )

    there = (has_prev, has_next)

    def send_halo(it):
        for t in range(tiles):
            at = slice(t * L, (t + 1) * L)
            hi, lo = split(mass[at, :] * vcur[at, :])
            field[at, 0:L] = hi
            field[at, L : 2 * L] = lo
        for side in range(2):
            packed = jnp.zeros((grows, L), F32)
            for j in range(groups):
                at = side * ghost + j * grows
                got = dot(ohs[at : at + grows, :], field[0:rows, :])
                got = (got[:, 0:L] + got[:, L:]) * mask[
                    fold0 + at : fold0 + at + grows, :
                ].astype(F32)
                packed = jnp.where(lane_group == j, replicate(got), packed)
            halo_send[it, side] = packed

            @pl.when(there[side])
            def _():
                halo_copy(it, side).start()

    def doubled(x):
        low = jnp.concatenate([x[:, 0:L], jnp.zeros((x.shape[0], L), x.dtype)], axis=1)
        return jnp.concatenate([x, low], axis=0)

    def project(it):
        got = dot(ohs[2 * ghost : 2 * ghost + slots, :], field[0:rows, :]).astype(BF)
        keep = mask[sup0 : sup0 + slots, :]
        got = got * jnp.concatenate([keep, keep], axis=1)
        part = dot(pa[...], doubled(got))
        part = replicate(part[:, 0:L] + part[:, L:])
        quarter = arows // groups
        group = lax.broadcasted_iota(jnp.int32, (quarter, L), 1) // cols
        packed = jnp.zeros((quarter, L), F32)
        for j in range(groups):
            packed = jnp.where(group == j, part[j * quarter : (j + 1) * quarter, :], packed)
        proj_send[it] = packed
        for k in range(1, n_col):
            proj_copy(it, k).start()

    def spread(it):
        for k in range(1, n_col):
            proj_copy(it, k).wait_recv()
        packed = proj_send[it]
        for k in range(1, n_col):
            packed = packed + proj_recv[it, k - 1]
        quarter = arows // groups
        group = lax.broadcasted_iota(jnp.int32, (quarter, L), 1) // cols
        for j in range(groups):
            at = slice(j * quarter, (j + 1) * quarter)
            part = replicate(jnp.where(group == j, packed, 0.0)) * cpl[at, :]
            coef[at, :] = part
        hi, lo = split(coef[...])
        back = dot(pat[...], doubled(jnp.concatenate([hi, lo], axis=1)))
        store(back[:, 0:L] + back[:, L:], sup0)

    def store(y, at):
        n = y.shape[0]
        keep = mask[pl.ds(at, n), :]
        hi, lo = split(y)
        z[pl.ds(at, n), 0:L] = hi * keep
        z[pl.ds(at, n), L : 2 * L] = lo * keep

    batch = cfg["batch"]

    def cell_step(gather_ref, first_cell, step):
        depth = gather_ref.shape[1]
        c0 = first_cell + step * batch
        local = pl.multiple_of(step * (batch * L), L)
        at = pl.multiple_of(c0 * L, L)
        got = dot(gather_ref[pl.ds(local, batch * L), :], field[0:depth, :]).astype(BF)
        keep = mask[pl.ds(at, batch * L), :]
        got = got * jnp.concatenate([keep, keep], axis=1)
        for u in range(batch):
            y = dot(smat[...], doubled(got[u * L : (u + 1) * L, :]))
            y = replicate((y[:, 0:L] + y[:, L:]) * scale_ref[c0 + u])
            store(y, pl.multiple_of(at + u * L, L))

    def cell_loop(gather_ref, first_cell, lo, hi):
        def step(s, carry):
            cell_step(gather_ref, first_cell, s)
            return carry

        lax.fori_loop(lo, hi, step, 0)

    def build_cells(lo, hi, gather_ref, ghosts_ref):
        def step(c, carry):
            local = pl.multiple_of((c - lo) * L, L)
            tables(
                cellrow[pl.ds(c, 1), :], pl.multiple_of(c * L, L), gather_ref, local,
                ghosts_ref, local,
            )
            return carry

        lax.fori_loop(lo, hi, step, 0)

    def build_atoms():
        paf[...] = jnp.zeros_like(paf)
        for t in range(slots // L):
            at = slice(t * L, (t + 1) * L)
            here = jnp.broadcast_to(atom_ref[t : t + 1, :], (nproj, L))
            values = proj_ref[:, at]
            for a in range(atoms):
                paf[a * nproj : (a + 1) * nproj, at] = jnp.where(here == a, values, 0.0)
        hi, lo = split(paf[0:arows, :])
        pa[:, 0:slots] = hi
        pa[:, slots : 2 * slots] = lo
        hi, lo = split(paf[...].T)
        pat[:, 0:apad] = hi
        pat[:, apad : 2 * apad] = lo
        for a in range(atoms):
            cpl[a * nproj : (a + 1) * nproj, :] = jnp.broadcast_to(
                coup_ref[:, a : a + 1], (nproj, L)
            )
        coef[...] = jnp.zeros_like(coef)

    send_halo(0)
    build_atoms()
    project(0)
    build_cells(0, inner, ohi, None)
    build_cells(inner, cells, ohb, otg)

    n_in = inner // batch
    n_out = (cells - inner) // batch
    early = cfg["early"]
    for it in range(2):
        if it > 0:
            send_halo(it)
            project(it)
        cell_loop(ohi, 0, 0, early)
        for side in range(2):
            @pl.when(there[side])
            def _():
                halo_copy(it, 1 - side).wait_recv()

            hi, lo = split(halo_recv[it, side])
            at = rows + side * grows
            field[at : at + grows, 0:L] = hi
            field[at : at + grows, L : 2 * L] = lo
        cell_loop(ohb, inner, 0, n_out)
        back = dot(otg[...], z[inner * L : cells * L, :])
        back = back[:, 0:L] + back[:, L:]
        for side in range(2):
            back_send[it, side] = back[side * grows : (side + 1) * grows, :]

            @pl.when(there[side])
            def _():
                back_copy(it, side).start()
        cell_loop(ohi, 0, early, n_in)
        spread(it)
        acc[...] = jnp.zeros_like(acc)
        chunk = cfg["chunk"]

        def scatter(s, carry):
            at = pl.multiple_of(s * chunk, chunk)
            acc[...] += dot(otm[:, pl.ds(at, chunk)], z[pl.ds(at, chunk), :])
            return carry

        lax.fori_loop(0, fold0 // chunk, scatter, 0)
        for side in range(2):
            @pl.when(there[side])
            def _():
                back_copy(it, 1 - side).wait_recv()

            packed = back_recv[it, side]
            for j in range(groups):
                store(
                    replicate(jnp.where(lane_group == j, packed, 0.0)),
                    fold0 + side * ghost + j * grows,
                )
        lax.fori_loop(fold0 // chunk, total // chunk, scatter, 0)
        for t in range(tiles):
            at = slice(t * L, (t + 1) * L)
            v = vcur[at, :]
            hv = mass[at, :] * (acc[at, 0:L] + acc[at, L:]) + pot[at, :] * v
            if it == 0:
                vcur[at, :] = (hv - 2.0 * v) * 0.25
            else:
                block = ((hv - 2.0 * v) * 0.5 - vwave[at, :]).T
                for q in range(groups):
                    out_ref[:, q * rows + t * L : q * rows + (t + 1) * L] = block[
                        q * cols : (q + 1) * cols, :
                    ]

    for it in range(2):
        for side in range(2):
            @pl.when(there[side])
            def _():
                halo_copy(it, side).wait_send()
                back_copy(it, side).wait_send()
        for k in range(1, n_col):
            proj_copy(it, k).wait_send()


def body(
    n_dom, n_col, wave, mass_scale, potential, stiffness, cell_scale, cell_map,
    send_left, send_right, support_node, support_atom, projector, coupling,
):
    nodes, cols = wave.shape
    ghost = send_left.shape[0]
    slots = support_node.shape[0]
    cells = cell_scale.shape[0]
    nproj, atoms = coupling.shape
    groups = L // cols
    rows = nodes // groups
    grows = ghost // groups
    inner = cells - cells // 4
    total = cells * L + slots + 2 * ghost
    arows = atoms * nproj
    apad = -(-arows // L) * L
    cfg = dict(
        n_dom=n_dom, n_col=n_col, cols=cols, groups=groups, rows=rows, cells=cells,
        inner=inner, cell_nodes=cell_map.shape[0], nodes=nodes, ghost=ghost, slots=slots,
        atoms=atoms, nproj=nproj, batch=4, early=3, chunk=512,
    )
    vm = pl.BlockSpec(memory_space=pltpu.VMEM)
    sm = pl.BlockSpec(memory_space=pltpu.SMEM)
    dma = pltpu.SemaphoreType.DMA
    out = pl.pallas_call(
        functools.partial(kernel, cfg),
        out_shape=jax.ShapeDtypeStruct((cols, nodes), F32),
        in_specs=[vm, vm, vm, vm, sm] + [vm] * 7,
        out_specs=vm,
        scratch_shapes=[
            pltpu.VMEM((rows + 2 * grows, 2 * L), BF),
            pltpu.VMEM((rows, L), F32),
            pltpu.VMEM((rows, L), F32),
            pltpu.VMEM((rows, L), F32),
            pltpu.VMEM((rows, L), F32),
            pltpu.VMEM((L, 2 * L), BF),
            pltpu.VMEM((cells, L), jnp.int32),
            pltpu.VMEM((inner * L, rows), BF),
            pltpu.VMEM(((cells - inner) * L, rows + 2 * grows), BF),
            pltpu.VMEM((2 * ghost + slots, rows), BF),
            pltpu.VMEM((rows, total), BF),
            pltpu.VMEM((2 * grows, (cells - inner) * L), BF),
            pltpu.VMEM((total, L), BF),
            pltpu.VMEM((total, 2 * L), BF),
            pltpu.VMEM((rows, 2 * L), F32),
            pltpu.VMEM((apad, slots), F32),
            pltpu.VMEM((arows, 2 * slots), BF),
            pltpu.VMEM((slots, 2 * apad), BF),
            pltpu.VMEM((arows, L), F32),
            pltpu.VMEM((apad, L), F32),
            pltpu.VMEM((2, 2, grows, L), F32),
            pltpu.VMEM((2, 2, grows, L), F32),
            pltpu.VMEM((2, 2, grows, L), F32),
            pltpu.VMEM((2, 2, grows, L), F32),
            pltpu.VMEM((2, arows // groups, L), F32),
            pltpu.VMEM((2, n_col - 1, arows // groups, L), F32),
            dma((2, 2)), dma((2, 2)), dma((2, 2)), dma((2, 2)),
            dma((2, n_col - 1)), dma((2, n_col - 1)),
        ],
        compiler_params=pltpu.CompilerParams(collective_id=0, has_side_effects=True),
        name="filter",
    )(
        wave.T, mass_scale.reshape(-1, L), potential.reshape(-1, L), stiffness, cell_scale,
        cell_map.T, send_left.reshape(-1, L), send_right.reshape(-1, L),
        support_node.reshape(-1, L), support_atom.reshape(-1, L), projector, coupling,
    )
    return out.T


def solution(mesh):
    both = ("dom", "col")
    return jax.shard_map(
        functools.partial(body, mesh.shape["dom"], mesh.shape["col"]),
        mesh=mesh,
        in_specs=(
            P(both, None), P(both), P(both), P(), P(both), P(None, both), P(both), P(both),
            P(both), P(both), P(None, both), P(None, "dom"),
        ),
        out_specs=P(both, None),
        check_vma=False,
    )
```

```python
import functools

import jax
import jax.numpy as jnp
from jax import lax
from jax.experimental import pallas as pl
from jax.experimental.pallas import tpu as pltpu
from jax.sharding import PartitionSpec as P

L = 128
BF = jnp.bfloat16
F32 = jnp.float32
MESH = pl.DeviceIdType.MESH


def split(x):
    hi = x.astype(BF)
    return hi, (x - hi.astype(F32)).astype(BF)


def dot(a, b):
    return jnp.dot(a, b, preferred_element_type=F32)


def kernel(
    cfg,
    wave_ref, mass_ref, pot_ref, stiff_ref, scale_ref, map_ref,
    left_ref, right_ref, node_ref, atom_ref, proj_ref, coup_ref,
    out_hbm,
    out_ref, field, vcur, vwave, mass, pot, smat, cellrow,
    ohi, ohb, ohs, otm, otg, mask, z, acc,
    paf, pa, pat, cpl, coef,
    halo_send, halo_recv, back_send, back_recv, proj_send, proj_recv,
    out_sem, hs_sem, hr_sem, bs_sem, br_sem, ps_sem, pr_sem,
):
    n_dom, n_col = cfg["n_dom"], cfg["n_col"]
    cols, groups, rows = cfg["cols"], cfg["groups"], cfg["rows"]
    cells, inner, width = cfg["cells"], cfg["inner"], cfg["cell_nodes"]
    nodes, ghost, slots = cfg["nodes"], cfg["ghost"], cfg["slots"]
    atoms, nproj = cfg["atoms"], cfg["nproj"]
    grows = ghost // groups
    tiles = rows // L
    far = 2 * rows
    sup0 = cells * L
    fold0 = sup0 + slots
    total = fold0 + 2 * ghost
    arows = atoms * nproj
    apad = paf.shape[0]

    dom = lax.axis_index("dom")
    col = lax.axis_index("col")
    me = dom * n_col + col
    last = n_dom * n_col - 1
    has_prev = me > 0
    has_next = me < last
    prev = jnp.maximum(me - 1, 0)
    after = jnp.minimum(me + 1, last)
    prev_id = (prev // n_col, prev % n_col)
    next_id = (after // n_col, after % n_col)
    outer_prev = jnp.logical_and(has_prev, col == 0)
    outer_next = jnp.logical_and(has_next, col == n_col - 1)

    zero_block = jnp.zeros((grows, L), F32)
    for it in range(2):
        @pl.when(jnp.logical_not(has_prev))
        def _():
            halo_recv[it, 0] = zero_block
            back_recv[it, 0] = zero_block

        @pl.when(jnp.logical_not(has_next))
        def _():
            halo_recv[it, 1] = zero_block
            back_recv[it, 1] = zero_block

    barrier = pltpu.get_barrier_semaphore()
    for k in range(1, n_col):
        pl.semaphore_signal(
            barrier, inc=1, device_id=(dom, (col + k) % n_col), device_id_type=MESH
        )

    @pl.when(outer_prev)
    def _():
        pl.semaphore_signal(barrier, inc=1, device_id=prev_id, device_id_type=MESH)

    @pl.when(outer_next)
    def _():
        pl.semaphore_signal(barrier, inc=1, device_id=next_id, device_id_type=MESH)

    lane = lax.broadcasted_iota(jnp.int32, (L, L), 1)
    sub = lax.broadcasted_iota(jnp.int32, (L, L), 0)
    lane_group = lane // cols

    def replicate(x):
        shift = L // 2
        while shift >= cols:
            x = x + pltpu.roll(x, shift, 1)
            shift //= 2
        return x

    for t in range(tiles):
        block = jnp.concatenate(
            [wave_ref[:, q * rows + t * L : q * rows + (t + 1) * L] for q in range(groups)], axis=0
        )
        block = block.T
        vcur[t * L : (t + 1) * L, :] = block
        vwave[t * L : (t + 1) * L, :] = block
        for source, target in ((mass_ref, mass), (pot_ref, pot)):
            block = jnp.concatenate(
                [
                    jnp.broadcast_to(source[q * tiles + t : q * tiles + t + 1, :], (cols, L))
                    for q in range(groups)
                ],
                axis=0,
            )
            target[t * L : (t + 1) * L, :] = block.T

    acc[0:L, 0:L] = jnp.zeros((L, L), F32)
    acc[0:width, 0:width] = stiff_ref[...]
    s_hi, s_lo = split(acc[0:L, 0:L])
    smat[:, 0:L] = s_hi
    smat[:, L : 2 * L] = s_lo

    def log2(x):
        return x.bit_length() - 1

    def place(n):
        g = n - nodes
        ghost_row = rows + ((g >> log2(ghost)) << log2(grows)) + (g & (grows - 1))
        ghost_code = (((g >> log2(grows)) & (groups - 1)) << log2(far)) + ghost_row
        owned_code = ((n >> log2(rows)) << log2(far)) + (n & (rows - 1))
        return jnp.where(n < 0, far - 1, jnp.where(g < 0, owned_code, ghost_code))

    cellrow[...] = jnp.full((cells, L), -1, jnp.int32)
    cellrow[:, 0:width] = map_ref[...]
    cellrow[...] = place(cellrow[...])

    def onehot(condition):
        return jnp.where(condition, 1.0, 0.0).astype(BF)

    def tables(row, at, gather_ref, gather_at, ghosts_ref=None, ghosts_at=0):
        wide = jnp.broadcast_to(row, (L, L))
        hi_r = wide & (far - 1)
        code = wide.T
        hi_c, q_c = code & (far - 1), code >> log2(far)
        for t in range(gather_ref.shape[1] // L):
            gather_ref[pl.ds(gather_at, L), t * L : (t + 1) * L] = onehot(hi_c == lane + t * L)
        mask[pl.ds(at, L), :] = onehot(q_c == lane_group)
        for t in range(tiles):
            otm[t * L : (t + 1) * L, pl.ds(at, L)] = onehot(hi_r == sub + t * L)
        if ghosts_ref is not None:
            for t in range(2 * grows // L):
                ghosts_ref[t * L : (t + 1) * L, pl.ds(ghosts_at, L)] = onehot(
                    hi_r == sub + (rows + t * L)
                )

    for k, ref in enumerate((left_ref, right_ref, node_ref)):
        base = (fold0, fold0 + ghost, sup0)[k]
        for t in range(ref.shape[0]):
            tables(place(ref[t : t + 1, :]), base + t * L, ohs, k * ghost + t * L)

    pl.semaphore_wait(
        barrier, n_col - 1 + jnp.where(outer_prev, 1, 0) + jnp.where(outer_next, 1, 0)
    )

    def halo_copy(it, side):
        return pltpu.make_async_remote_copy(
            src_ref=halo_send.at[it, side], dst_ref=halo_recv.at[it, 1 - side],
            send_sem=hs_sem.at[it, side], recv_sem=hr_sem.at[it, 1 - side],
            device_id=(prev_id, next_id)[side], device_id_type=MESH,
        )

    def back_copy(it, side):
        return pltpu.make_async_remote_copy(
            src_ref=back_send.at[it, side], dst_ref=back_recv.at[it, 1 - side],
            send_sem=bs_sem.at[it, side], recv_sem=br_sem.at[it, 1 - side],
            device_id=(prev_id, next_id)[side], device_id_type=MESH,
        )

    def proj_copy(it, k):
        return pltpu.make_async_remote_copy(
            src_ref=proj_send.at[it], dst_ref=proj_recv.at[it, k - 1],
            send_sem=ps_sem.at[it, k - 1], recv_sem=pr_sem.at[it, k - 1],
            device_id=(dom, (col + k) % n_col), device_id_type=MESH,
        )

    there = (has_prev, has_next)

    def send_halo(it):
        for t in range(tiles):
            at = slice(t * L, (t + 1) * L)
            hi, lo = split(mass[at, :] * vcur[at, :])
            field[at, 0:L] = hi
            field[at, L : 2 * L] = lo
        for side in range(2):
            packed = jnp.zeros((grows, L), F32)
            for j in range(groups):
                at = side * ghost + j * grows
                got = dot(ohs[at : at + grows, :], field[0:rows, :])
                got = (got[:, 0:L] + got[:, L:]) * mask[
                    fold0 + at : fold0 + at + grows, :
                ].astype(F32)
                packed = jnp.where(lane_group == j, replicate(got), packed)
            halo_send[it, side] = packed

            @pl.when(there[side])
            def _():
                halo_copy(it, side).start()

    def doubled(x):
        low = jnp.concatenate([x[:, 0:L], jnp.zeros((x.shape[0], L), x.dtype)], axis=1)
        return jnp.concatenate([x, low], axis=0)

    def project(it):
        got = dot(ohs[2 * ghost : 2 * ghost + slots, :], field[0:rows, :]).astype(BF)
        keep = mask[sup0 : sup0 + slots, :]
        got = got * jnp.concatenate([keep, keep], axis=1)
        part = dot(pa[...], doubled(got))
        part = replicate(part[:, 0:L] + part[:, L:])
        quarter = arows // groups
        group = lax.broadcasted_iota(jnp.int32, (quarter, L), 1) // cols
        packed = jnp.zeros((quarter, L), F32)
        for j in range(groups):
            packed = jnp.where(group == j, part[j * quarter : (j + 1) * quarter, :], packed)
        proj_send[it] = packed
        for k in range(1, n_col):
            proj_copy(it, k).start()

    def spread(it):
        for k in range(1, n_col):
            proj_copy(it, k).wait_recv()
        packed = proj_send[it]
        for k in range(1, n_col):
            packed = packed + proj_recv[it, k - 1]
        quarter = arows // groups
        group = lax.broadcasted_iota(jnp.int32, (quarter, L), 1) // cols
        for j in range(groups):
            at = slice(j * quarter, (j + 1) * quarter)
            part = replicate(jnp.where(group == j, packed, 0.0)) * cpl[at, :]
            coef[at, :] = part
        hi, lo = split(coef[...])
        back = dot(pat[...], doubled(jnp.concatenate([hi, lo], axis=1)))
        store(back[:, 0:L] + back[:, L:], sup0)

    def store(y, at):
        n = y.shape[0]
        keep = mask[pl.ds(at, n), :]
        hi, lo = split(y)
        z[pl.ds(at, n), 0:L] = hi * keep
        z[pl.ds(at, n), L : 2 * L] = lo * keep

    batch = cfg["batch"]

    def cell_step(gather_ref, first_cell, step):
        depth = gather_ref.shape[1]
        c0 = first_cell + step * batch
        local = pl.multiple_of(step * (batch * L), L)
        at = pl.multiple_of(c0 * L, L)
        got = dot(gather_ref[pl.ds(local, batch * L), :], field[0:depth, :]).astype(BF)
        keep = mask[pl.ds(at, batch * L), :]
        got = got * jnp.concatenate([keep, keep], axis=1)
        for u in range(batch):
            y = dot(smat[...], doubled(got[u * L : (u + 1) * L, :]))
            y = replicate((y[:, 0:L] + y[:, L:]) * scale_ref[c0 + u])
            store(y, pl.multiple_of(at + u * L, L))

    def cell_loop(gather_ref, first_cell, lo, hi):
        def step(s, carry):
            cell_step(gather_ref, first_cell, s)
            return carry

        lax.fori_loop(lo, hi, step, 0)

    def build_cells(lo, hi, gather_ref, ghosts_ref):
        def step(c, carry):
            local = pl.multiple_of((c - lo) * L, L)
            tables(
                cellrow[pl.ds(c, 1), :], pl.multiple_of(c * L, L), gather_ref, local,
                ghosts_ref, local,
            )
            return carry

        lax.fori_loop(lo, hi, step, 0)

    def build_atoms():
        paf[...] = jnp.zeros_like(paf)
        for t in range(slots // L):
            at = slice(t * L, (t + 1) * L)
            here = jnp.broadcast_to(atom_ref[t : t + 1, :], (nproj, L))
            values = proj_ref[:, at]
            for a in range(atoms):
                paf[a * nproj : (a + 1) * nproj, at] = jnp.where(here == a, values, 0.0)
        hi, lo = split(paf[0:arows, :])
        pa[:, 0:slots] = hi
        pa[:, slots : 2 * slots] = lo
        hi, lo = split(paf[...].T)
        pat[:, 0:apad] = hi
        pat[:, apad : 2 * apad] = lo
        for a in range(atoms):
            cpl[a * nproj : (a + 1) * nproj, :] = jnp.broadcast_to(
                coup_ref[:, a : a + 1], (nproj, L)
            )
        coef[...] = jnp.zeros_like(coef)

    send_halo(0)
    build_atoms()
    project(0)
    build_cells(0, inner, ohi, None)
    build_cells(inner, cells, ohb, otg)

    n_in = inner // batch
    n_out = (cells - inner) // batch
    early = cfg["early"]
    for it in range(2):
        if it > 0:
            send_halo(it)
            project(it)
        cell_loop(ohi, 0, 0, early)
        for side in range(2):
            @pl.when(there[side])
            def _():
                halo_copy(it, 1 - side).wait_recv()

            hi, lo = split(halo_recv[it, side])
            at = rows + side * grows
            field[at : at + grows, 0:L] = hi
            field[at : at + grows, L : 2 * L] = lo
        cell_loop(ohb, inner, 0, n_out)
        back = dot(otg[...], z[inner * L : cells * L, :])
        back = back[:, 0:L] + back[:, L:]
        for side in range(2):
            back_send[it, side] = back[side * grows : (side + 1) * grows, :]

            @pl.when(there[side])
            def _():
                back_copy(it, side).start()
        cell_loop(ohi, 0, early, n_in)
        spread(it)
        acc[...] = jnp.zeros_like(acc)
        chunk = cfg["chunk"]

        def scatter(s, carry):
            at = pl.multiple_of(s * chunk, chunk)
            acc[...] += dot(otm[:, pl.ds(at, chunk)], z[pl.ds(at, chunk), :])
            return carry

        lax.fori_loop(0, fold0 // chunk, scatter, 0)
        for side in range(2):
            @pl.when(there[side])
            def _():
                back_copy(it, 1 - side).wait_recv()

            packed = back_recv[it, side]
            for j in range(groups):
                store(
                    replicate(jnp.where(lane_group == j, packed, 0.0)),
                    fold0 + side * ghost + j * grows,
                )
        acc[...] += dot(otm[:, fold0:total], z[fold0:total, :])
        for t in range(tiles):
            at = slice(t * L, (t + 1) * L)
            v = vcur[at, :]
            hv = mass[at, :] * (acc[at, 0:L] + acc[at, L:]) + pot[at, :] * v
            if it == 0:
                vcur[at, :] = (hv - 2.0 * v) * 0.25
            else:
                block = ((hv - 2.0 * v) * 0.5 - vwave[at, :]).T
                for q in range(groups):
                    out_ref[:, q * rows + t * L : q * rows + (t + 1) * L] = block[
                        q * cols : (q + 1) * cols, :
                    ]

    done = pltpu.make_async_copy(out_ref, out_hbm, out_sem)
    done.start()
    for it in range(2):
        for side in range(2):
            @pl.when(there[side])
            def _():
                halo_copy(it, side).wait_send()
                back_copy(it, side).wait_send()
        for k in range(1, n_col):
            proj_copy(it, k).wait_send()
    done.wait()


def body(
    n_dom, n_col, wave, mass_scale, potential, stiffness, cell_scale, cell_map,
    send_left, send_right, support_node, support_atom, projector, coupling,
):
    nodes, cols = wave.shape
    ghost = send_left.shape[0]
    slots = support_node.shape[0]
    cells = cell_scale.shape[0]
    nproj, atoms = coupling.shape
    groups = L // cols
    rows = nodes // groups
    grows = ghost // groups
    inner = cells - cells // 4
    total = cells * L + slots + 2 * ghost
    arows = atoms * nproj
    apad = -(-arows // L) * L
    cfg = dict(
        n_dom=n_dom, n_col=n_col, cols=cols, groups=groups, rows=rows, cells=cells,
        inner=inner, cell_nodes=cell_map.shape[0], nodes=nodes, ghost=ghost, slots=slots,
        atoms=atoms, nproj=nproj, batch=8, early=1, chunk=1536,
    )
    vm = pl.BlockSpec(memory_space=pltpu.VMEM)
    sm = pl.BlockSpec(memory_space=pltpu.SMEM)
    dma = pltpu.SemaphoreType.DMA
    out = pl.pallas_call(
        functools.partial(kernel, cfg),
        out_shape=jax.ShapeDtypeStruct((cols, nodes), F32),
        in_specs=[vm, vm, vm, vm, sm] + [vm] * 7,
        out_specs=pl.BlockSpec(memory_space=pltpu.HBM),
        scratch_shapes=[
            pltpu.VMEM((cols, nodes), F32),
            pltpu.VMEM((rows + 2 * grows, 2 * L), BF),
            pltpu.VMEM((rows, L), F32),
            pltpu.VMEM((rows, L), F32),
            pltpu.VMEM((rows, L), F32),
            pltpu.VMEM((rows, L), F32),
            pltpu.VMEM((L, 2 * L), BF),
            pltpu.VMEM((cells, L), jnp.int32),
            pltpu.VMEM((inner * L, rows), BF),
            pltpu.VMEM(((cells - inner) * L, rows + 2 * grows), BF),
            pltpu.VMEM((2 * ghost + slots, rows), BF),
            pltpu.VMEM((rows, total), BF),
            pltpu.VMEM((2 * grows, (cells - inner) * L), BF),
            pltpu.VMEM((total, L), BF),
            pltpu.VMEM((total, 2 * L), BF),
            pltpu.VMEM((rows, 2 * L), F32),
            pltpu.VMEM((apad, slots), F32),
            pltpu.VMEM((arows, 2 * slots), BF),
            pltpu.VMEM((slots, 2 * apad), BF),
            pltpu.VMEM((arows, L), F32),
            pltpu.VMEM((apad, L), F32),
            pltpu.VMEM((2, 2, grows, L), F32),
            pltpu.VMEM((2, 2, grows, L), F32),
            pltpu.VMEM((2, 2, grows, L), F32),
            pltpu.VMEM((2, 2, grows, L), F32),
            pltpu.VMEM((2, arows // groups, L), F32),
            pltpu.VMEM((2, n_col - 1, arows // groups, L), F32),
            dma(()), dma((2, 2)), dma((2, 2)), dma((2, 2)), dma((2, 2)),
            dma((2, n_col - 1)), dma((2, n_col - 1)),
        ],
        compiler_params=pltpu.CompilerParams(collective_id=0, has_side_effects=True),
        name="filter",
    )(
        wave.T, mass_scale.reshape(-1, L), potential.reshape(-1, L), stiffness, cell_scale,
        cell_map.T, send_left.reshape(-1, L), send_right.reshape(-1, L),
        support_node.reshape(-1, L), support_atom.reshape(-1, L), projector, coupling,
    )
    return out.T


def solution(mesh):
    both = ("dom", "col")
    return jax.shard_map(
        functools.partial(body, mesh.shape["dom"], mesh.shape["col"]),
        mesh=mesh,
        in_specs=(
            P(both, None), P(both), P(both), P(), P(both), P(None, both), P(both), P(both),
            P(both), P(both), P(None, both), P(None, "dom"),
        ),
        out_specs=P(both, None),
        check_vma=False,
    )
```
